1024 devices in a mesh: replica: 64 (over z_hi, y, x), tensor: 16 (over z_lo, core).
Axes of the slice: x: 4, y: 8, z: 16 (z_hi: 2, z_lo: 8; z = z_hi * 8 + z_lo), core: 2. Of those that a mesh axis runs over, the one named last changes fastest.
Arguments:
- train_hidden: bfloat16 [1024, 14784], P(None, 'replica'), may hold values from -6 to 6
- out_grad: bfloat16 [1024, 4096], P('tensor'), may hold values from -6 to 6
- master: float32 [14784, 4096], P('replica', 'tensor'), may hold values from -0.046875 to 0.046875
- first_moment: float32 [14784, 4096], P('replica', 'tensor'), may hold values from -6 to 6
- second_moment: float32 [14784, 4096], P('replica', 'tensor'), may hold values from 0.25 to 4
- decode_hidden: bfloat16 [16384, 14784], P('replica'), may hold values from -6 to 6
Outputs:
- new_master: float32 [14784, 4096], P('replica', 'tensor')
- new_first: float32 [14784, 4096], P('replica', 'tensor')
- new_second: float32 [14784, 4096], P('replica', 'tensor')
- decoded: bfloat16 [16384, 4096], P('replica', 'tensor')
The draws below stay inside these ranges and needn't reach their ends.
All inputs are finite; a program needn't handle non-finite values.
Results may differ from the reference program's by a relative error of at most 0.0049.
Values may be sent and summed in bfloat16 or wider, within the bound.
A program may use at most 64 MiB of HBM per device.

```python
import math
import jax
import jax.numpy as jnp
from jax import lax

D = 4096
FF = 14784
TOK = 1024
ROWS_ALL = 16384


def block_levels(stream_key, dims, shards, smallest, largest):
    factor_of = 1.0
    for axis_at, shards_of in shards:
        draws = jax.random.uniform(jax.random.fold_in(jax.random.fold_in(stream_key, 6), axis_at), (shards_of,), jnp.float32, smallest / len(shards), largest / len(shards))
        factor_of = factor_of * jnp.repeat(jnp.exp(draws), dims[axis_at] // shards_of).reshape((-1,) + (1,) * (len(dims) - 1 - axis_at))
    return factor_of


def noise(stream_key, dims, deviation, reach, shards=(), dtype=jnp.bfloat16):
    array = deviation * jax.random.normal(stream_key, dims, jnp.float32)
    if shards:
        array = array * block_levels(stream_key, dims, shards, -0.22, 0.18)
    return jnp.clip(array, -reach, reach).astype(dtype)


def setup_inputs(seed: int = 0) -> dict:
    streams_of = jax.random.split(jax.random.key(seed), 7)
    return {
        "train_hidden": noise(streams_of[0], (TOK, FF), 1.0, 6.0, ((1, 64),)),
        "out_grad": noise(streams_of[1], (TOK, D), 1.0, 6.0, ((0, 16),)),
        "master": noise(streams_of[2], (FF, D), FF ** -0.5, 0.046875, ((0, 64), (1, 16)), jnp.float32),
        "first_moment": noise(streams_of[3], (FF, D), 1.0, 6.0, ((0, 64), (1, 16)), jnp.float32),
        "second_moment": jnp.clip(jnp.exp(math.log(4.0) - 2.7725887 * jax.random.uniform(streams_of[4], (FF, D), jnp.float32) ** block_levels(streams_of[4], (FF, D), ((0, 64), (1, 16)), -0.2, 0.2)), 0.25, 4.0),
        "decode_hidden": noise(streams_of[5], (ROWS_ALL, FF), 1.0, 6.0, ((0, 64),)),
    }


def reference(train_hidden, out_grad, master, first_moment, second_moment, decode_hidden):
    grad = lax.dot_general(train_hidden, out_grad, (((0,), (0,)), ((), ())), preferred_element_type=jnp.float32)
    grad = grad * (1.0 / math.sqrt(TOK))
    new_first = 0.9 * first_moment + 0.1 * grad
    new_second = 0.95 * second_moment + 0.05 * grad * grad
    new_master = master - 0.002 * new_first / (jnp.sqrt(new_second) + 1e-08)
    weights = new_master.astype(jnp.bfloat16)
    decoded = jnp.dot(decode_hidden, weights, preferred_element_type=jnp.float32).astype(jnp.bfloat16)
    return (new_master, new_first, new_second, decoded)
```

```python
import math

import jax
import jax.numpy as jnp
from jax import lax
from jax.experimental import pallas as pl
from jax.experimental.pallas import tpu as pltpu
from jax.sharding import PartitionSpec as P

MESH = pl.DeviceIdType.MESH
NX, NY, NZ = 4, 8, 16
HALF = NZ // 2
SLOT = 256
SENT = 240
CUT = 96
PARTS = ((0, CUT), (CUT, SENT - CUT))
RELAY_AFTER = 2
LAG = 4


def offsets(hops):
    out = []
    for i in (0, 1, -1, 2):
        j = hops - abs(i)
        if j == 0:
            out.append((i, 0))
        elif j > 0:
            if j <= NY // 2:
                out.append((i, j))
            if j <= NY // 2 - 1:
                out.append((i, -j))
    return out


def kernel(
    th_hbm, og_hbm, ma_hbm, fi_hbm, se_hbm, dh_hbm,
    nm_hbm, nf_hbm, ns_hbm, dec_hbm,
    th, og, cols, ma, fi, se, nm, nf, ns, wide, dh, apad, w, relay, acc, dec,
    in_sem, out_sem, col_send, col_recv, own_sem, w_send, w_recv, z_send, z_recv,
):
    r = lax.axis_index("replica")
    t = lax.axis_index("tensor")
    x, y, zh = r % NX, (r // NX) % NY, r // (NX * NY)
    zl, core = t // 2, t % 2
    z = zh * HALF + zl
    rows, width = ma.shape
    tokens_in = og.shape[0]
    tokens_all = th.shape[0]

    def device(xx, yy, zz, cc):
        return ((zz // HALF) * (NX * NY) + yy * NX + xx, (zz % HALF) * 2 + cc)

    loads = [
        pltpu.make_async_copy(a, b, in_sem.at[k])
        for k, (a, b) in enumerate(
            ((og_hbm, og), (dh_hbm, dh), (th_hbm, th), (ma_hbm, ma), (fi_hbm, fi), (se_hbm, se))
        )
    ]
    for copy in loads:
        copy.start()

    right, left = (x + 1) % NX, (x + NX - 1) % NX
    up, down = (y + 1) % NY, (y + NY - 1) % NY
    barrier = pltpu.get_barrier_semaphore()
    greeted = [device(right, y, z, core), device(left, y, z, core),
               device(x, up, z, core), device(x, down, z, core), device(x, y, z, 1 - core)]
    for d in (4, -4, 3, -3, 2, -2, 1, -1):
        for c in range(2):
            greeted.append(device(x, y, (z + d + NZ) % NZ, c))
    for d in reversed(greeted):
        pl.semaphore_signal(barrier, inc=1, device_id=d, device_id_type=MESH)
    pl.semaphore_wait(barrier, len(greeted))

    loads[0].wait()
    first = pl.multiple_of(zl * 2 * tokens_in + core * tokens_in, tokens_in)
    own = pltpu.make_async_copy(
        og.at[:, pl.ds(pl.multiple_of(t * width, width), width)],
        cols.at[pl.ds(first, tokens_in)], own_sem)
    own.start()

    def send_columns(d, c, lo, n):
        zz = (z + d + NZ) % NZ
        tt = (zz % HALF) * 2 + c
        pltpu.make_async_remote_copy(
            src_ref=og.at[pl.ds(lo, n), pl.ds(pl.multiple_of(tt * width, width), width)],
            dst_ref=cols.at[pl.ds(pl.multiple_of(first + lo, n), n)],
            send_sem=col_send, recv_sem=col_recv,
            device_id=device(x, y, zz, c), device_id_type=MESH,
        ).start()

    half = tokens_in // 2
    for c in range(2):
        send_columns(4, c, 0, half)
        send_columns(-4, c, half, half)
    for d in (3, -3, 2, -2, 1, -1):
        for c in range(2):
            send_columns(d, c, 0, tokens_in)
    send_columns(0, 1 - core, 0, tokens_in)

    wide[...] = jnp.zeros_like(wide)
    acc[...] = jnp.zeros_like(acc)

    def clear(g, carry):
        for k in range(NX):
            w[g, pl.ds(k * SLOT + SENT, SLOT - SENT), :] = jnp.zeros((SLOT - SENT, width), w.dtype)
        return carry

    lax.fori_loop(0, w.shape[0], clear, 0)
    loads[1].wait()
    strip = 64
    lane = lax.broadcasted_iota(jnp.int32, (strip, 128), 1)

    def place(b, tiles, shift, strip_at):
        turned = [pltpu.roll(v.astype(jnp.float32), (128 - shift) % 128, 1) for v in tiles]
        low = jnp.where(lane < 128 - shift, turned[0], turned[1])
        high = jnp.where(lane < 128 - shift, turned[1], turned[2])
        high = jnp.where(lane < rows - 128, high, 0.0)
        at = pl.multiple_of((b % NX) * SLOT, SLOT)
        apad[b // NX, pl.ds(strip_at, strip), pl.ds(at, 128)] = low.astype(apad.dtype)
        apad[b // NX, pl.ds(strip_at, strip), pl.ds(pl.multiple_of(at + 128, 128), 128)] = high.astype(apad.dtype)

    blocks = NX * w.shape[0]

    def relayout(b, carry):
        base = (b * rows) // 128 * 128
        shift = b * rows - base
        for s in range(0, dh.shape[0], strip):
            tiles = [dh[pl.ds(s, strip), pl.ds(pl.multiple_of(base + 128 * k, 128), 128)] for k in range(3)]
            place(b, tiles, shift, s)
        return carry

    lax.fori_loop(0, blocks - 1, relayout, 0)
    last = (blocks - 1) * rows
    tail = dh.shape[1] - last // 128 * 128 - 256
    for s in range(0, dh.shape[0], strip):
        base = last // 128 * 128
        tiles = [dh[pl.ds(s, strip), pl.ds(base + 128 * k, 128)] for k in range(2)]
        tiles.append(jnp.concatenate(
            [dh[pl.ds(s, strip), pl.ds(base + 256, tail)], jnp.zeros((strip, 128 - tail), dh.dtype)], axis=1))
        place(blocks - 1, tiles, last - base, s)

    for copy in loads[2:]:
        copy.wait()
    own.wait()
    others = tokens_all - tokens_in
    pltpu.make_async_copy(cols.at[pl.ds(0, others)], cols.at[pl.ds(0, others)], col_recv).wait()
    grad = lax.dot_general(th[...], cols[...], (((0,), (0,)), ((), ())), preferred_element_type=jnp.float32)
    grad = grad * (1.0 / math.sqrt(tokens_all))
    new_first = 0.9 * fi[...] + 0.1 * grad
    new_second = 0.95 * se[...] + 0.05 * grad * grad
    new_master = ma[...] - 0.002 * new_first / (jnp.sqrt(new_second) + 1e-08)
    wide[pl.ds(0, rows), :] = new_master

    def slot_of(ref, b, lo, n):
        return ref.at[b // NX, pl.ds(pl.multiple_of((b % NX) * SLOT + lo, 16), n)]

    w[r // NX, pl.ds(pl.multiple_of((r % NX) * SLOT, SLOT), SENT), :] = wide[pl.ds(0, SENT), :].astype(w.dtype)

    def geometry(s):
        sign = 1 - 2 * ((core + s) % 2)
        plane = (zh + s) % 2

        def block(i, j):
            xx = (x - i * sign + 2 * NX) % NX
            yy = (y - j * sign + 2 * NY) % NY
            return plane * (NX * NY) + yy * NX + xx

        def toward(axis, step):
            if axis == 0:
                return device((x + step * sign + NX) % NX, y, z, core)
            return device(x, (y + step * sign + NY) % NY, z, core)

        return block, toward

    def forward(b, part, to):
        lo, n = PARTS[part]
        pltpu.make_async_remote_copy(
            src_ref=slot_of(w, b, lo, n), dst_ref=slot_of(w, b, lo, n),
            send_sem=w_send, recv_sem=w_recv.at[b * 2 + part], device_id=to, device_id_type=MESH,
        ).start()

    def arrived(b, part):
        lo, n = PARTS[part]
        pltpu.make_async_copy(slot_of(w, b, lo, n), slot_of(w, b, lo, n), w_recv.at[b * 2 + part]).wait()

    def onward(s, i, j, part):
        block, toward = geometry(s)
        b = block(i, j)
        first_axis = 0 if part == 0 else 1
        along = (i, j)[first_axis]
        across = (i, j)[1 - first_axis]
        reach = (NX // 2, NY // 2)
        if across == 0:
            if 0 <= along < reach[first_axis]:
                forward(b, part, toward(first_axis, 1))
            if -(reach[first_axis] - 1) < along <= 0:
                forward(b, part, toward(first_axis, -1))
        if 0 <= across < reach[1 - first_axis]:
            forward(b, part, toward(1 - first_axis, 1))
        if -(reach[1 - first_axis] - 1) < across <= 0:
            forward(b, part, toward(1 - first_axis, -1))

    def wave(s, hops):
        block, _ = geometry(s)
        for i, j in offsets(hops):
            for part in ((1, 0) if i == 0 else (0, 1)):
                arrived(block(i, j), part)
                onward(s, i, j, part)

    def multiply(s, j):
        block, _ = geometry(s)
        g = block(0, j) // NX
        acc[...] += jnp.dot(apad[g], w[g], preferred_element_type=jnp.float32)

    def multiply_after(s, hops):
        j = hops - 2
        if j == 0:
            multiply(s, 0)
        elif 0 < j < NY // 2:
            def both(k, carry):
                multiply(s, j * (1 - 2 * k))
                return carry
            lax.fori_loop(0, 2, both, 0)
        elif j == NY // 2:
            multiply(s, j)

    zs = 4 * (1 - 2 * core)
    steps = (zs, -zs)
    for part, (lo, n) in enumerate(PARTS):
        pltpu.make_async_remote_copy(
            src_ref=slot_of(w, r, lo, n), dst_ref=relay.at[pl.ds(lo, n)],
            send_sem=z_send.at[part], recv_sem=z_recv.at[part],
            device_id=device(x, y, (z + steps[part] + NZ) % NZ, core), device_id_type=MESH,
        ).start()
    for part in (1, 0):
        onward(0, 0, 0, part)
    outs = [
        pltpu.make_async_copy(a, b, out_sem.at[k])
        for k, (a, b) in enumerate(((nm, nm_hbm), (nf, nf_hbm), (ns, ns_hbm)))
    ]
    nm[...] = new_master
    nf[...] = new_first
    ns[...] = new_second
    for copy in outs:
        copy.start()

    def serve_relay():
        for part, (lo, n) in enumerate(PARTS):
            origin = (z - steps[part] + NZ) % NZ
            target = (z + steps[part] + NZ) % NZ
            b = (origin // HALF) * (NX * NY) + y * NX + x
            pltpu.make_async_copy(relay.at[pl.ds(lo, n)], relay.at[pl.ds(lo, n)], z_recv.at[part]).wait()
            pltpu.make_async_remote_copy(
                src_ref=relay.at[pl.ds(lo, n)], dst_ref=slot_of(w, b, lo, n),
                send_sem=z_send.at[2 + part], recv_sem=w_recv.at[b * 2 + part],
                device_id=device(x, y, target, core), device_id_type=MESH,
            ).start()

    far = NX // 2 + NY // 2
    for hops in range(1, far + LAG):
        if hops == LAG:
            block, _ = geometry(1)
            for part in (1, 0):
                arrived(block(0, 0), part)
                onward(1, 0, 0, part)
        if hops <= far:
            wave(0, hops)
        if hops == RELAY_AFTER:
            serve_relay()
        if 1 <= hops - LAG + 1 <= far and hops >= LAG:
            wave(1, hops - LAG + 1)
        if hops <= far:
            multiply_after(0, hops)
        if hops >= LAG:
            multiply_after(1, hops - LAG + 1)

    dec[...] = acc[...].astype(dec.dtype)
    final = pltpu.make_async_copy(dec, dec_hbm, out_sem.at[3])
    final.start()

    pltpu.make_async_copy(cols.at[pl.ds(0, others)], cols.at[pl.ds(0, others)], col_send).wait()
    for k in range(4):
        lo, n = PARTS[k % 2]
        pltpu.make_async_copy(relay.at[pl.ds(lo, n)], relay.at[pl.ds(lo, n)], z_send.at[k]).wait()
    window = w.at[pl.ds(0, 2 * NY - 1), pl.ds(0, 2 * (NX * NY - 1) * SENT // (2 * NY - 1))]
    pltpu.make_async_copy(window, window, w_send).wait()
    for copy in outs:
        copy.wait()
    final.wait()


def per_device(train_hidden, out_grad, master, first_moment, second_moment, decode_hidden):
    rows, width = master.shape
    tokens_all = train_hidden.shape[0]
    lines = decode_hidden.shape[0]
    f32, bf16 = jnp.float32, jnp.bfloat16
    any_spec = pl.BlockSpec(memory_space=pl.ANY)
    block = jax.ShapeDtypeStruct((rows, width), f32)
    groups = 2 * NY
    return pl.pallas_call(
        kernel,
        out_shape=(block, block, block, jax.ShapeDtypeStruct((lines, width), bf16)),
        in_specs=[any_spec] * 6,
        out_specs=(any_spec,) * 4,
        scratch_shapes=[
            pltpu.VMEM(train_hidden.shape, bf16),
            pltpu.VMEM(out_grad.shape, bf16),
            pltpu.VMEM((tokens_all, width), bf16),
            pltpu.VMEM((rows, width), f32),
            pltpu.VMEM((rows, width), f32),
            pltpu.VMEM((rows, width), f32),
            pltpu.VMEM((rows, width), f32),
            pltpu.VMEM((rows, width), f32),
            pltpu.VMEM((rows, width), f32),
            pltpu.VMEM((SLOT, width), f32),
            pltpu.VMEM(decode_hidden.shape, bf16),
            pltpu.VMEM((groups, lines, NX * SLOT), bf16),
            pltpu.VMEM((groups, NX * SLOT, width), bf16),
            pltpu.VMEM((SENT, width), bf16),
            pltpu.VMEM((lines, width), f32),
            pltpu.VMEM((lines, width), bf16),
            pltpu.SemaphoreType.DMA((6,)),
            pltpu.SemaphoreType.DMA((4,)),
            pltpu.SemaphoreType.DMA,
            pltpu.SemaphoreType.DMA,
            pltpu.SemaphoreType.DMA,
            pltpu.SemaphoreType.DMA,
            pltpu.SemaphoreType.DMA((2 * NX * groups,)),
            pltpu.SemaphoreType.DMA((4,)),
            pltpu.SemaphoreType.DMA((2,)),
        ],
        compiler_params=pltpu.CompilerParams(
            collective_id=0, has_side_effects=True, vmem_limit_bytes=60 * 1024 * 1024
        ),
    )(train_hidden, out_grad, master, first_moment, second_moment, decode_hidden)


def solution(mesh):
    placed = (
        P(None, "replica"),
        P("tensor", None),
        P("replica", "tensor"),
        P("replica", "tensor"),
        P("replica", "tensor"),
        P("replica", None),
    )
    return jax.shard_map(
        per_device,
        mesh=mesh,
        in_specs=placed,
        out_specs=(
            P("replica", "tensor"),
            P("replica", "tensor"),
            P("replica", "tensor"),
            P("replica", "tensor"),
        ),
        check_vma=False,
    )
```

```python
import math

import jax
import jax.numpy as jnp
from jax import lax
from jax.experimental import pallas as pl
from jax.experimental.pallas import tpu as pltpu
from jax.sharding import PartitionSpec as P

MESH = pl.DeviceIdType.MESH
NX, NY, NZ = 4, 8, 16
HALF = NZ // 2
SLOT = 256
SENT = 240
CUT = 96
PARTS = ((0, CUT), (CUT, SENT - CUT))
RELAY_AFTER = 1
LAG = 4


def offsets(hops):
    out = []
    for i in (0, 1, -1, 2):
        j = hops - abs(i)
        if j == 0:
            out.append((i, 0))
        elif j > 0:
            if j <= NY // 2:
                out.append((i, j))
            if j <= NY // 2 - 1:
                out.append((i, -j))
    return out


def kernel(
    th_hbm, og_hbm, ma_hbm, fi_hbm, se_hbm, dh_hbm,
    nm_hbm, nf_hbm, ns_hbm, dec_hbm,
    th, og, cols, ma, fi, se, nm, nf, ns, wide, dh, apad, w, relay, acc, dec,
    in_sem, out_sem, col_send, col_recv, own_sem, w_send, w_recv, z_send, z_recv,
):
    r = lax.axis_index("replica")
    t = lax.axis_index("tensor")
    x, y, zh = r % NX, (r // NX) % NY, r // (NX * NY)
    zl, core = t // 2, t % 2
    z = zh * HALF + zl
    rows, width = ma.shape
    tokens_in = og.shape[0]
    tokens_all = th.shape[1]

    def device(xx, yy, zz, cc):
        return ((zz // HALF) * (NX * NY) + yy * NX + xx, (zz % HALF) * 2 + cc)

    loads = [
        pltpu.make_async_copy(a, b, in_sem.at[k])
        for k, (a, b) in enumerate(
            ((og_hbm, og), (dh_hbm, dh.at[pl.ds(0, dh_hbm.shape[0])]), (th_hbm, th), (ma_hbm, ma), (fi_hbm, fi), (se_hbm, se))
        )
    ]
    for copy in loads:
        copy.start()

    right, left = (x + 1) % NX, (x + NX - 1) % NX
    up, down = (y + 1) % NY, (y + NY - 1) % NY
    barrier = pltpu.get_barrier_semaphore()
    greeted = [device(right, y, z, core), device(left, y, z, core),
               device(x, up, z, core), device(x, down, z, core), device(x, y, z, 1 - core)]
    for d in (4, -4, 3, -3, 2, -2, 1, -1):
        for c in range(2):
            greeted.append(device(x, y, (z + d + NZ) % NZ, c))
    for d in reversed(greeted):
        pl.semaphore_signal(barrier, inc=1, device_id=d, device_id_type=MESH)
    pl.semaphore_wait(barrier, len(greeted))

    loads[0].wait()
    first = pl.multiple_of(zl * 2 * tokens_in + core * tokens_in, tokens_in)
    own = pltpu.make_async_copy(
        og.at[:, pl.ds(pl.multiple_of(t * width, width), width)],
        cols.at[pl.ds(first, tokens_in)], own_sem)
    own.start()

    def send_columns(d, c, lo, n):
        zz = (z + d + NZ) % NZ
        tt = (zz % HALF) * 2 + c
        pltpu.make_async_remote_copy(
            src_ref=og.at[pl.ds(lo, n), pl.ds(pl.multiple_of(tt * width, width), width)],
            dst_ref=cols.at[pl.ds(pl.multiple_of(first + lo, n), n)],
            send_sem=col_send, recv_sem=col_recv,
            device_id=device(x, y, zz, c), device_id_type=MESH,
        ).start()

    half = tokens_in // 2
    for c in range(2):
        send_columns(4, c, 0, half)
        send_columns(-4, c, half, half)
    for d in (3, -3, 2, -2, 1, -1):
        for c in range(2):
            send_columns(d, c, 0, tokens_in)
    send_columns(0, 1 - core, 0, tokens_in)

    wide[...] = jnp.zeros_like(wide)
    acc[...] = jnp.zeros_like(acc)

    def clear(g, carry):
        for k in range(NX):
            w[g, pl.ds(k * SLOT + SENT, SLOT - SENT), :] = jnp.zeros((SLOT - SENT, width), w.dtype)
        return carry

    lax.fori_loop(0, w.shape[0], clear, 0)
    loads[1].wait()
    lane = lax.broadcasted_iota(jnp.int32, (128, 128), 1)

    def relayout(b, carry):
        base = pl.multiple_of((b * rows) // 16 * 16, 16)
        shift = b * rows - base
        at = pl.multiple_of((b % NX) * SLOT, SLOT)
        for s in range(0, dh.shape[1], 128):
            tile = dh[pl.ds(base, SLOT), pl.ds(s, 128)].T.astype(jnp.float32)
            turned = [pltpu.roll(tile[:, k * 128 : k * 128 + 128], (128 - shift) % 128, 1) for k in range(2)]
            low = jnp.where(lane < 128 - shift, turned[0], turned[1])
            high = jnp.where(lane < rows - 128, turned[1], 0.0)
            apad[b // NX, pl.ds(s, 128), pl.ds(at, 128)] = low.astype(apad.dtype)
            apad[b // NX, pl.ds(s, 128), pl.ds(pl.multiple_of(at + 128, 128), 128)] = high.astype(apad.dtype)
        return carry

    lax.fori_loop(0, NX * w.shape[0], relayout, 0)

    for copy in loads[2:]:
        copy.wait()
    own.wait()
    others = tokens_all - tokens_in
    pltpu.make_async_copy(cols.at[pl.ds(0, others)], cols.at[pl.ds(0, others)], col_recv).wait()
    grad = jnp.dot(th[...], cols[...], preferred_element_type=jnp.float32)
    grad = grad * (1.0 / math.sqrt(tokens_all))
    new_first = 0.9 * fi[...] + 0.1 * grad
    new_second = 0.95 * se[...] + 0.05 * grad * grad
    new_master = ma[...] - 0.002 * new_first / (jnp.sqrt(new_second) + 1e-08)
    wide[pl.ds(0, rows), :] = new_master

    def slot_of(ref, b, lo, n):
        return ref.at[b // NX, pl.ds(pl.multiple_of((b % NX) * SLOT + lo, 16), n)]

    w[r // NX, pl.ds(pl.multiple_of((r % NX) * SLOT, SLOT), SENT), :] = wide[pl.ds(0, SENT), :].astype(w.dtype)

    def geometry(s):
        sign = 1 - 2 * ((core + s) % 2)
        plane = (zh + s) % 2

        def block(i, j):
            xx = (x - i * sign + 2 * NX) % NX
            yy = (y - j * sign + 2 * NY) % NY
            return plane * (NX * NY) + yy * NX + xx

        def toward(axis, step):
            if axis == 0:
                return device((x + step * sign + NX) % NX, y, z, core)
            return device(x, (y + step * sign + NY) % NY, z, core)

        return block, toward

    def forward(b, part, to):
        lo, n = PARTS[part]
        pltpu.make_async_remote_copy(
            src_ref=slot_of(w, b, lo, n), dst_ref=slot_of(w, b, lo, n),
            send_sem=w_send, recv_sem=w_recv.at[b * 2 + part], device_id=to, device_id_type=MESH,
        ).start()

    def arrived(b, part):
        lo, n = PARTS[part]
        pltpu.make_async_copy(slot_of(w, b, lo, n), slot_of(w, b, lo, n), w_recv.at[b * 2 + part]).wait()

    def onward(s, i, j, part):
        block, toward = geometry(s)
        b = block(i, j)
        first_axis = 0 if part == 0 else 1
        along = (i, j)[first_axis]
        across = (i, j)[1 - first_axis]
        reach = (NX // 2, NY // 2)
        if across == 0:
            if 0 <= along < reach[first_axis]:
                forward(b, part, toward(first_axis, 1))
            if -(reach[first_axis] - 1) < along <= 0:
                forward(b, part, toward(first_axis, -1))
        if 0 <= across < reach[1 - first_axis]:
            forward(b, part, toward(1 - first_axis, 1))
        if -(reach[1 - first_axis] - 1) < across <= 0:
            forward(b, part, toward(1 - first_axis, -1))

    def wave(s, hops):
        block, _ = geometry(s)
        for i, j in offsets(hops):
            for part in ((1, 0) if i == 0 else (0, 1)):
                arrived(block(i, j), part)
                onward(s, i, j, part)

    def multiply(s, j):
        block, _ = geometry(s)
        g = block(0, j) // NX
        acc[...] += jnp.dot(apad[g], w[g], preferred_element_type=jnp.float32)

    def multiply_after(s, hops):
        j = hops - 2
        if j == 0:
            multiply(s, 0)
        elif 0 < j < NY // 2:
            def both(k, carry):
                multiply(s, j * (1 - 2 * k))
                return carry
            lax.fori_loop(0, 2, both, 0)
        elif j == NY // 2:
            multiply(s, j)

    zs = 4 * (1 - 2 * core)
    steps = (zs, -zs)
    for part, (lo, n) in enumerate(PARTS):
        pltpu.make_async_remote_copy(
            src_ref=slot_of(w, r, lo, n), dst_ref=relay.at[pl.ds(lo, n)],
            send_sem=z_send.at[part], recv_sem=z_recv.at[part],
            device_id=device(x, y, (z + steps[part] + NZ) % NZ, core), device_id_type=MESH,
        ).start()
    for part in (1, 0):
        onward(0, 0, 0, part)
    outs = [
        pltpu.make_async_copy(a, b, out_sem.at[k])
        for k, (a, b) in enumerate(((nm, nm_hbm), (nf, nf_hbm), (ns, ns_hbm)))
    ]
    nm[...] = new_master
    nf[...] = new_first
    ns[...] = new_second
    for copy in outs:
        copy.start()

    def serve_relay():
        for part, (lo, n) in enumerate(PARTS):
            origin = (z - steps[part] + NZ) % NZ
            target = (z + steps[part] + NZ) % NZ
            b = (origin // HALF) * (NX * NY) + y * NX + x
            pltpu.make_async_copy(relay.at[pl.ds(lo, n)], relay.at[pl.ds(lo, n)], z_recv.at[part]).wait()
            pltpu.make_async_remote_copy(
                src_ref=relay.at[pl.ds(lo, n)], dst_ref=slot_of(w, b, lo, n),
                send_sem=z_send.at[2 + part], recv_sem=w_recv.at[b * 2 + part],
                device_id=device(x, y, target, core), device_id_type=MESH,
            ).start()

    far = NX // 2 + NY // 2
    for hops in range(1, far + LAG):
        if hops == LAG:
            block, _ = geometry(1)
            for part in (1, 0):
                arrived(block(0, 0), part)
                onward(1, 0, 0, part)
        if hops <= far:
            wave(0, hops)
        if hops == RELAY_AFTER:
            serve_relay()
        if 1 <= hops - LAG + 1 <= far and hops >= LAG:
            wave(1, hops - LAG + 1)
        if hops <= far:
            multiply_after(0, hops)
        if hops >= LAG:
            multiply_after(1, hops - LAG + 1)

    dec[...] = acc[...].astype(dec.dtype)
    final = pltpu.make_async_copy(dec, dec_hbm, out_sem.at[3])
    final.start()

    pltpu.make_async_copy(cols.at[pl.ds(0, others)], cols.at[pl.ds(0, others)], col_send).wait()
    for k in range(4):
        lo, n = PARTS[k % 2]
        pltpu.make_async_copy(relay.at[pl.ds(lo, n)], relay.at[pl.ds(lo, n)], z_send.at[k]).wait()
    window = w.at[pl.ds(0, 2 * NY - 1), pl.ds(0, 2 * (NX * NY - 1) * SENT // (2 * NY - 1))]
    pltpu.make_async_copy(window, window, w_send).wait()
    for copy in outs:
        copy.wait()
    final.wait()


def hand_on(*refs):
    for source, target in zip(refs[:4], refs[4:]):
        target[...] = source[...]


def per_device(train_hidden, out_grad, master, first_moment, second_moment, decode_hidden):
    rows, width = master.shape
    tokens_all = train_hidden.shape[0]
    lines = decode_hidden.shape[0]
    f32, bf16 = jnp.float32, jnp.bfloat16
    any_spec = pl.BlockSpec(memory_space=pl.ANY)
    block = jax.ShapeDtypeStruct((rows, width), f32)
    groups = 2 * NY
    results = pl.pallas_call(
        kernel,
        out_shape=(block, block, block, jax.ShapeDtypeStruct((lines, width), bf16)),
        in_specs=[any_spec] * 6,
        out_specs=(any_spec,) * 4,
        scratch_shapes=[
            pltpu.VMEM((rows, tokens_all), bf16),
            pltpu.VMEM(out_grad.shape, bf16),
            pltpu.VMEM((tokens_all, width), bf16),
            pltpu.VMEM((rows, width), f32),
            pltpu.VMEM((rows, width), f32),
            pltpu.VMEM((rows, width), f32),
            pltpu.VMEM((rows, width), f32),
            pltpu.VMEM((rows, width), f32),
            pltpu.VMEM((rows, width), f32),
            pltpu.VMEM((SLOT, width), f32),
            pltpu.VMEM((decode_hidden.shape[1] + 16, lines), bf16),
            pltpu.VMEM((groups, lines, NX * SLOT), bf16),
            pltpu.VMEM((groups, NX * SLOT, width), bf16),
            pltpu.VMEM((SENT, width), bf16),
            pltpu.VMEM((lines, width), f32),
            pltpu.VMEM((lines, width), bf16),
            pltpu.SemaphoreType.DMA((6,)),
            pltpu.SemaphoreType.DMA((4,)),
            pltpu.SemaphoreType.DMA,
            pltpu.SemaphoreType.DMA,
            pltpu.SemaphoreType.DMA,
            pltpu.SemaphoreType.DMA,
            pltpu.SemaphoreType.DMA((2 * NX * groups,)),
            pltpu.SemaphoreType.DMA((4,)),
            pltpu.SemaphoreType.DMA((2,)),
        ],
        compiler_params=pltpu.CompilerParams(
            collective_id=0, has_side_effects=True, vmem_limit_bytes=60 * 1024 * 1024
        ),
    )(train_hidden.T, out_grad, master, first_moment, second_moment, decode_hidden.T)
    return pl.pallas_call(
        hand_on,
        out_shape=tuple(jax.ShapeDtypeStruct(a.shape, a.dtype) for a in results),
    )(*results)


def solution(mesh):
    placed = (
        P(None, "replica"),
        P("tensor", None),
        P("replica", "tensor"),
        P("replica", "tensor"),
        P("replica", "tensor"),
        P("replica", None),
    )
    return jax.shard_map(
        per_device,
        mesh=mesh,
        in_specs=placed,
        out_specs=(
            P("replica", "tensor"),
            P("replica", "tensor"),
            P("replica", "tensor"),
            P("replica", "tensor"),
        ),
        check_vma=False,
    )
```

```python
import math

import jax
import jax.numpy as jnp
from jax import lax
from jax.experimental import pallas as pl
from jax.experimental.pallas import tpu as pltpu
from jax.sharding import PartitionSpec as P

MESH = pl.DeviceIdType.MESH
NX, NY, NZ = 4, 8, 16
HALF = NZ // 2
SLOT = 256
SENT = 232
CUT = 96
PARTS = ((0, CUT), (CUT, SENT - CUT))
RELAY_AFTER = 1
LAG = 5


def offsets(hops):
    out = []
    for i in (0, 1, -1, 2):
        j = hops - abs(i)
        if j == 0:
            out.append((i, 0))
        elif j > 0:
            if j <= NY // 2:
                out.append((i, j))
            if j <= NY // 2 - 1:
                out.append((i, -j))
    return out


def kernel(
    th_hbm, og_hbm, ma_hbm, fi_hbm, se_hbm, dh_hbm,
    nm_hbm, nf_hbm, ns_hbm, dec_hbm,
    th, og, cols, ma, fi, se, nm, nf, ns, wide, dh, apad, w, relay, acc, dec,
    in_sem, out_sem, col_send, col_recv, x_send, x_recv, own_sem, everyone, w_send, w_recv, z_send, z_recv,
):
    r = lax.axis_index("replica")
    t = lax.axis_index("tensor")
    x, y, zh = r % NX, (r // NX) % NY, r // (NX * NY)
    zl, core = t // 2, t % 2
    z = zh * HALF + zl
    rows, width = ma.shape
    tokens_in = og.shape[0]
    tokens_all = th.shape[1]

    def device(xx, yy, zz, cc):
        return ((zz // HALF) * (NX * NY) + yy * NX + xx, (zz % HALF) * 2 + cc)

    loads = [
        pltpu.make_async_copy(a, b, in_sem.at[k])
        for k, (a, b) in enumerate(
            ((og_hbm, og), (dh_hbm, dh.at[pl.ds(0, dh_hbm.shape[0])]), (th_hbm, th), (ma_hbm, ma), (fi_hbm, fi), (se_hbm, se))
        )
    ]
    for copy in loads:
        copy.start()

    right, left = (x + 1) % NX, (x + NX - 1) % NX
    up, down = (y + 1) % NY, (y + NY - 1) % NY
    barrier = pltpu.get_barrier_semaphore()
    greeted = [device(right, y, z, core), device(left, y, z, core),
               device(x, up, z, core), device(x, down, z, core), device(x, y, z, 1 - core)]
    for d in range(1, HALF):
        zz = zh * HALF + (zl + d) % HALF
        for c in range(2):
            greeted.append(device(x, y, zz, c))
    for d in greeted:
        pl.semaphore_signal(barrier, inc=1, device_id=d, device_id_type=MESH)

    lane = lax.broadcasted_iota(jnp.int32, (128, 128), 1)

    def relayout(b):
        base = pl.multiple_of((b * rows) // 16 * 16, 16)
        shift = b * rows - base
        at = pl.multiple_of((b % NX) * SLOT, SLOT)
        for s in range(0, dh.shape[1], 128):
            tile = dh[pl.ds(base, SLOT), pl.ds(s, 128)].T.astype(jnp.float32)
            turned = [pltpu.roll(tile[:, k * 128 : k * 128 + 128], (128 - shift) % 128, 1) for k in range(2)]
            low = jnp.where(lane < 128 - shift, turned[0], turned[1])
            high = jnp.where(lane < rows - 128, turned[1], 0.0)
            apad[b // NX, pl.ds(s, 128), pl.ds(at, 128)] = low.astype(apad.dtype)
            apad[b // NX, pl.ds(s, 128), pl.ds(pl.multiple_of(at + 128, 128), 128)] = high.astype(apad.dtype)

    def relayout_plane(plane, lo, n):
        def one(k, carry):
            relayout(plane * (NX * NY) + lo + k)
            return carry
        lax.fori_loop(0, n, one, 0)

    def clear(g, carry):
        for k in range(NX):
            w[g, pl.ds(k * SLOT + SENT, SLOT - SENT), :] = jnp.zeros((SLOT - SENT, width), w.dtype)
        return carry

    def prepare():
        loads[1].wait()
        lax.fori_loop(0, w.shape[0], clear, 0)
        relayout_plane(zh, 0, NX * NY)

    early = (z < HALF // 2) | (z == HALF)
    pl.when(early)(prepare)

    pl.semaphore_wait(barrier, len(greeted) + (z == HALF).astype(jnp.int32))

    @pl.when(z == HALF - 1)
    def _():
        pl.semaphore_signal(barrier, inc=1, device_id=device(x, y, HALF, core), device_id_type=MESH)

    @pl.when(z == HALF)
    def _():
        for d in range(1, NZ):
            pl.semaphore_signal(everyone, inc=1, device_id=device(x, y, (HALF + d) % NZ, core), device_id_type=MESH)

    loads[0].wait()
    quarter = tokens_in // NX
    mine = pl.ds(pl.multiple_of(x * quarter, quarter), quarter)
    own = pltpu.make_async_copy(og.at[mine, pl.ds(pl.multiple_of(t * width, width), width)], cols.at[t, mine], own_sem)
    own.start()

    def send_columns(d, c):
        zz = zh * HALF + (zl + d) % HALF
        tt = (zz % HALF) * 2 + c
        pltpu.make_async_remote_copy(
            src_ref=og.at[mine, pl.ds(pl.multiple_of(tt * width, width), width)],
            dst_ref=cols.at[t, mine],
            send_sem=col_send, recv_sem=col_recv,
            device_id=device(x, y, zz, c), device_id_type=MESH,
        ).start()

    for d in range(1, HALF):
        for c in range(2):
            send_columns(HALF - d, c)
    send_columns(0, 1 - core)

    wide[...] = jnp.zeros_like(wide)
    acc[...] = jnp.zeros_like(acc)
    pl.when(jnp.logical_not(early))(prepare)

    own.wait()
    peers = cols.at[pl.ds(0, cols.shape[0] - 1), pl.ds(0, quarter)]
    pltpu.make_async_copy(peers, peers, col_recv).wait()

    def quarters(xx, lo, n):
        return cols.at[pl.ds(lo, n), pl.ds(pl.multiple_of(xx * quarter, quarter), quarter)]

    sources = cols.shape[0]
    half = sources // 2

    def pass_on(xx, lo, n, to, k):
        pltpu.make_async_remote_copy(
            src_ref=quarters(xx, lo, n), dst_ref=quarters(xx, lo, n),
            send_sem=x_send.at[k], recv_sem=x_recv.at[k],
            device_id=device(to, y, z, core), device_id_type=MESH,
        ).start()

    def passed(xx, lo, n, sem):
        pltpu.make_async_copy(quarters(xx, lo, n), quarters(xx, lo, n), sem).wait()

    opposite = (x + 2) % NX
    pass_on(x, 0, sources, right, 0)
    pass_on(x, 0, sources, left, 1)
    passed(left, 0, sources, x_recv.at[0])
    pass_on(left, 0, half, right, 2)
    passed(right, 0, sources, x_recv.at[1])
    pass_on(right, half, half, left, 3)

    for copy in loads[2:]:
        copy.wait()
    passed(opposite, 0, half, x_recv.at[2])
    passed(opposite, half, half, x_recv.at[3])
    grad = jnp.dot(th[...], cols[...].reshape(tokens_all, width), preferred_element_type=jnp.float32)
    grad = grad * (1.0 / math.sqrt(tokens_all))
    new_first = 0.9 * fi[...] + 0.1 * grad
    new_second = 0.95 * se[...] + 0.05 * grad * grad
    new_master = ma[...] - 0.002 * new_first / (jnp.sqrt(new_second) + 1e-08)
    wide[pl.ds(0, rows), :] = new_master

    def slot_of(ref, b, lo, n):
        return ref.at[b // NX, pl.ds(pl.multiple_of((b % NX) * SLOT + lo, 16), n)]

    w[r // NX, pl.ds(pl.multiple_of((r % NX) * SLOT, SLOT), SENT), :] = wide[pl.ds(0, SENT), :].astype(w.dtype)

    def geometry(s):
        sign = 1 - 2 * ((core + s) % 2)
        plane = (zh + s) % 2

        def block(i, j):
            xx = (x - i * sign + 2 * NX) % NX
            yy = (y - j * sign + 2 * NY) % NY
            return plane * (NX * NY) + yy * NX + xx

        def toward(axis, step):
            if axis == 0:
                return device((x + step * sign + NX) % NX, y, z, core)
            return device(x, (y + step * sign + NY) % NY, z, core)

        return block, toward

    def forward(b, part, to):
        lo, n = PARTS[part]
        pltpu.make_async_remote_copy(
            src_ref=slot_of(w, b, lo, n), dst_ref=slot_of(w, b, lo, n),
            send_sem=w_send, recv_sem=w_recv.at[b * 2 + part], device_id=to, device_id_type=MESH,
        ).start()

    def arrived(b, part):
        lo, n = PARTS[part]
        pltpu.make_async_copy(slot_of(w, b, lo, n), slot_of(w, b, lo, n), w_recv.at[b * 2 + part]).wait()

    def onward(s, i, j, part):
        block, toward = geometry(s)
        b = block(i, j)
        first_axis = 0 if part == 0 else 1
        along = (i, j)[first_axis]
        across = (i, j)[1 - first_axis]
        reach = (NX // 2, NY // 2)
        if across == 0:
            if 0 <= along < reach[first_axis]:
                forward(b, part, toward(first_axis, 1))
            if -(reach[first_axis] - 1) < along <= 0:
                forward(b, part, toward(first_axis, -1))
        if 0 <= across < reach[1 - first_axis]:
            forward(b, part, toward(1 - first_axis, 1))
        if -(reach[1 - first_axis] - 1) < across <= 0:
            forward(b, part, toward(1 - first_axis, -1))

    def wave(s, hops):
        block, _ = geometry(s)
        for i, j in offsets(hops):
            for part in ((1, 0) if i == 0 else (0, 1)):
                arrived(block(i, j), part)
                onward(s, i, j, part)

    def multiply(s, j):
        block, _ = geometry(s)
        g = block(0, j) // NX
        acc[...] += jnp.dot(apad[g], w[g], preferred_element_type=jnp.float32)

    def multiply_after(s, hops):
        j = hops - 2
        if j == 0:
            multiply(s, 0)
        elif 0 < j < NY // 2:
            def both(k, carry):
                multiply(s, j * (1 - 2 * k))
                return carry
            lax.fori_loop(0, 2, both, 0)
        elif j == NY // 2:
            multiply(s, j)

    for part in (1, 0):
        onward(0, 0, 0, part)

    @pl.when(z != HALF)
    def _():
        pl.semaphore_wait(everyone, 1)

    zs = 4 * (1 - 2 * core)
    steps = (zs, -zs)
    for part, (lo, n) in enumerate(PARTS):
        pltpu.make_async_remote_copy(
            src_ref=slot_of(w, r, lo, n), dst_ref=relay.at[pl.ds(lo, n)],
            send_sem=z_send.at[part], recv_sem=z_recv.at[part],
            device_id=device(x, y, (z + steps[part] + NZ) % NZ, core), device_id_type=MESH,
        ).start()
    outs = [
        pltpu.make_async_copy(a, b, out_sem.at[k])
        for k, (a, b) in enumerate(((nm, nm_hbm), (nf, nf_hbm), (ns, ns_hbm)))
    ]
    nm[...] = new_master
    nf[...] = new_first
    ns[...] = new_second
    for copy in outs:
        copy.start()

    def serve_relay():
        for part, (lo, n) in enumerate(PARTS):
            origin = (z - steps[part] + NZ) % NZ
            target = (z + steps[part] + NZ) % NZ
            b = (origin // HALF) * (NX * NY) + y * NX + x
            pltpu.make_async_copy(relay.at[pl.ds(lo, n)], relay.at[pl.ds(lo, n)], z_recv.at[part]).wait()
            pltpu.make_async_remote_copy(
                src_ref=relay.at[pl.ds(lo, n)], dst_ref=slot_of(w, b, lo, n),
                send_sem=z_send.at[2 + part], recv_sem=w_recv.at[b * 2 + part],
                device_id=device(x, y, target, core), device_id_type=MESH,
            ).start()

    far = NX // 2 + NY // 2
    for hops in range(1, far + LAG):
        if hops == LAG:
            block, _ = geometry(1)
            for part in (1, 0):
                arrived(block(0, 0), part)
                onward(1, 0, 0, part)
        if hops <= far:
            wave(0, hops)
        if hops == RELAY_AFTER:
            serve_relay()
        if 1 <= hops - LAG + 1 <= far and hops >= LAG:
            wave(1, hops - LAG + 1)
        if hops <= far:
            multiply_after(0, hops)
        if 2 <= hops < 2 + NY // 2:
            relayout_plane(1 - zh, (hops - 2) * 2 * NX, 2 * NX)
        if hops >= LAG:
            multiply_after(1, hops - LAG + 1)

    dec[...] = acc[...].astype(dec.dtype)
    final = pltpu.make_async_copy(dec, dec_hbm, out_sem.at[3])
    final.start()

    pltpu.make_async_copy(peers, peers, col_send).wait()
    for k, n in enumerate((sources, sources, half, half)):
        passed(0, 0, n, x_send.at[k])
    for k in range(4):
        lo, n = PARTS[k % 2]
        pltpu.make_async_copy(relay.at[pl.ds(lo, n)], relay.at[pl.ds(lo, n)], z_send.at[k]).wait()
    window = dh.at[pl.ds(0, 2 * (NX * NY - 1) * SENT)]
    pltpu.make_async_copy(window, window, w_send).wait()
    for copy in outs:
        copy.wait()
    final.wait()


def hand_on(*refs):
    for source, target in zip(refs[:4], refs[4:]):
        target[...] = source[...]


def per_device(train_hidden, out_grad, master, first_moment, second_moment, decode_hidden):
    rows, width = master.shape
    tokens_all = train_hidden.shape[0]
    lines = decode_hidden.shape[0]
    f32, bf16 = jnp.float32, jnp.bfloat16
    any_spec = pl.BlockSpec(memory_space=pl.ANY)
    block = jax.ShapeDtypeStruct((rows, width), f32)
    groups = 2 * NY
    results = pl.pallas_call(
        kernel,
        out_shape=(block, block, block, jax.ShapeDtypeStruct((lines, width), bf16)),
        in_specs=[any_spec] * 6,
        out_specs=(any_spec,) * 4,
        scratch_shapes=[
            pltpu.VMEM((rows, tokens_all), bf16),
            pltpu.VMEM(out_grad.shape, bf16),
            pltpu.VMEM((tokens_all // out_grad.shape[0], out_grad.shape[0], width), bf16),
            pltpu.VMEM((rows, width), f32),
            pltpu.VMEM((rows, width), f32),
            pltpu.VMEM((rows, width), f32),
            pltpu.VMEM((rows, width), f32),
            pltpu.VMEM((rows, width), f32),
            pltpu.VMEM((rows, width), f32),
            pltpu.VMEM((SLOT, width), f32),
            pltpu.VMEM((decode_hidden.shape[1] + 16, lines), bf16),
            pltpu.VMEM((groups, lines, NX * SLOT), bf16),
            pltpu.VMEM((groups, NX * SLOT, width), bf16),
            pltpu.VMEM((SENT, width), bf16),
            pltpu.VMEM((lines, width), f32),
            pltpu.VMEM((lines, width), bf16),
            pltpu.SemaphoreType.DMA((6,)),
            pltpu.SemaphoreType.DMA((4,)),
            pltpu.SemaphoreType.DMA,
            pltpu.SemaphoreType.DMA,
            pltpu.SemaphoreType.DMA((4,)),
            pltpu.SemaphoreType.DMA((4,)),
            pltpu.SemaphoreType.DMA,
            pltpu.SemaphoreType.REGULAR,
            pltpu.SemaphoreType.DMA,
            pltpu.SemaphoreType.DMA((2 * NX * groups,)),
            pltpu.SemaphoreType.DMA((4,)),
            pltpu.SemaphoreType.DMA((2,)),
        ],
        compiler_params=pltpu.CompilerParams(
            collective_id=0, has_side_effects=True, vmem_limit_bytes=60 * 1024 * 1024
        ),
    )(train_hidden.T, out_grad, master, first_moment, second_moment, decode_hidden.T)
    return pl.pallas_call(
        hand_on,
        out_shape=tuple(jax.ShapeDtypeStruct(a.shape, a.dtype) for a in results),
    )(*results)


def solution(mesh):
    placed = (
        P(None, "replica"),
        P("tensor", None),
        P("replica", "tensor"),
        P("replica", "tensor"),
        P("replica", "tensor"),
        P("replica", None),
    )
    return jax.shard_map(
        per_device,
        mesh=mesh,
        in_specs=placed,
        out_specs=(
            P("replica", "tensor"),
            P("replica", "tensor"),
            P("replica", "tensor"),
            P("replica", "tensor"),
        ),
        check_vma=False,
    )
```

```python
import math

import jax
import jax.numpy as jnp
from jax import lax
from jax.experimental import pallas as pl
from jax.experimental.pallas import tpu as pltpu
from jax.sharding import PartitionSpec as P

MESH = pl.DeviceIdType.MESH
NX, NY, NZ = 4, 8, 16
HALF = NZ // 2
SLOT = 256
SENT = 232
CUT = 96
PARTS = ((0, CUT), (CUT, SENT - CUT))
RELAY_AFTER = 1
LAG = 5


def offsets(hops):
    out = []
    for i in (0, 1, -1, 2):
        j = hops - abs(i)
        if j == 0:
            out.append((i, 0))
        elif j > 0:
            if j <= NY // 2:
                out.append((i, j))
            if j <= NY // 2 - 1:
                out.append((i, -j))
    return out


def kernel(
    th_hbm, og_hbm, ma_hbm, fi_hbm, se_hbm, dh_hbm,
    nm_hbm, nf_hbm, ns_hbm, dec_hbm,
    th, og, cols, ma, fi, se, nm, nf, ns, wide, dh, apad, w, relay, acc, dec,
    in_sem, out_sem, col_send, col_recv, x_send, x_recv, own_sem, upper_in, up_send, w_send, w_recv, z_send, z_recv,
):
    r = lax.axis_index("replica")
    t = lax.axis_index("tensor")
    x, y, zh = r % NX, (r // NX) % NY, r // (NX * NY)
    zl, core = t // 2, t % 2
    z = zh * HALF + zl
    rows, width = ma.shape
    tokens_in = og.shape[0]
    tokens_all = th.shape[1]

    def device(xx, yy, zz, cc):
        return ((zz // HALF) * (NX * NY) + yy * NX + xx, (zz % HALF) * 2 + cc)

    loads = [
        pltpu.make_async_copy(a, b, in_sem.at[k])
        for k, (a, b) in enumerate(
            ((og_hbm, og), (dh_hbm, dh.at[pl.ds(0, dh_hbm.shape[0])]), (th_hbm, th), (ma_hbm, ma), (fi_hbm, fi), (se_hbm, se))
        )
    ]
    for copy in loads:
        copy.start()

    right, left = (x + 1) % NX, (x + NX - 1) % NX
    up, down = (y + 1) % NY, (y + NY - 1) % NY
    barrier = pltpu.get_barrier_semaphore()
    greeted = [device(right, y, z, core), device(left, y, z, core),
               device(x, up, z, core), device(x, down, z, core), device(x, y, z, 1 - core)]
    lower = z < HALF
    upper = z >= HALF
    near = [(k, d, c) for k, d in enumerate((4, -4, 3, -3, 2, -2, 1, -1)) for c in range(2)]

    def along(d):
        return (z + d + NZ) % NZ

    for d in greeted:
        pl.semaphore_signal(barrier, inc=1, device_id=d, device_id_type=MESH)
    for k, d, c in near:
        @pl.when(along(d) >= HALF)
        def _():
            pl.semaphore_signal(barrier, inc=1, device_id=device(x, y, along(d), c), device_id_type=MESH)

    @pl.when(lower)
    def _():
        for d in range(1, HALF):
            for c in range(2):
                pl.semaphore_signal(barrier, inc=1, device_id=device(x, y, (z + d) % HALF, c), device_id_type=MESH)

    lane = lax.broadcasted_iota(jnp.int32, (128, 128), 1)

    def relayout(b):
        base = pl.multiple_of((b * rows) // 16 * 16, 16)
        shift = b * rows - base
        at = pl.multiple_of((b % NX) * SLOT, SLOT)
        for s in range(0, dh.shape[1], 128):
            tile = dh[pl.ds(base, SLOT), pl.ds(s, 128)].T.astype(jnp.float32)
            turned = [pltpu.roll(tile[:, k * 128 : k * 128 + 128], (128 - shift) % 128, 1) for k in range(2)]
            low = jnp.where(lane < 128 - shift, turned[0], turned[1])
            high = jnp.where(lane < rows - 128, turned[1], 0.0)
            apad[b // NX, pl.ds(s, 128), pl.ds(at, 128)] = low.astype(apad.dtype)
            apad[b // NX, pl.ds(s, 128), pl.ds(pl.multiple_of(at + 128, 128), 128)] = high.astype(apad.dtype)

    def relayout_plane(plane, lo, n):
        def one(k, carry):
            relayout(plane * (NX * NY) + lo + k)
            return carry
        lax.fori_loop(0, n, one, 0)

    def clear(g, carry):
        for k in range(NX):
            w[g, pl.ds(k * SLOT + SENT, SLOT - SENT), :] = jnp.zeros((SLOT - SENT, width), w.dtype)
        return carry

    def prepare():
        loads[1].wait()
        lax.fori_loop(0, w.shape[0], clear, 0)
        relayout_plane(zh, 0, NX * NY)

    early = z < HALF // 2
    pl.when(early)(prepare)

    pl.semaphore_wait(barrier, len(greeted) + 2 * jnp.where(lower, HALF - 1, HALF))
    for k, d, c in near:
        @pl.when(upper & (along(d) < HALF))
        def _():
            pl.semaphore_signal(upper_in, inc=1, device_id=device(x, y, along(d), c), device_id_type=MESH)

    loads[0].wait()
    quarter = tokens_in // NX
    mine = pl.ds(pl.multiple_of(x * quarter, quarter), quarter)
    own_columns = pl.ds(pl.multiple_of(t * width, width), width)
    own_part = pltpu.make_async_copy(og.at[mine, own_columns], cols.at[t, mine], own_sem)
    own_all = pltpu.make_async_copy(og.at[:, own_columns], cols.at[t], own_sem)

    def send_quarter(d, c):
        zz = (z + d) % HALF
        tt = zz * 2 + c
        pltpu.make_async_remote_copy(
            src_ref=og.at[mine, pl.ds(pl.multiple_of(tt * width, width), width)],
            dst_ref=cols.at[t, mine],
            send_sem=col_send, recv_sem=col_recv,
            device_id=device(x, y, zz, c), device_id_type=MESH,
        ).start()

    def whole(k, d, c):
        lo, n = {4: (0, tokens_in // 2), -4: (tokens_in // 2, tokens_in // 2)}.get(d, (0, tokens_in))
        tt = (along(d) % HALF) * 2 + c
        return pltpu.make_async_remote_copy(
            src_ref=og.at[pl.ds(lo, n), pl.ds(pl.multiple_of(tt * width, width), width)],
            dst_ref=cols.at[t, pl.ds(lo, n)],
            send_sem=up_send.at[2 * k + c], recv_sem=col_recv,
            device_id=device(x, y, along(d), c), device_id_type=MESH,
        )

    def whole_sibling():
        tt = zl * 2 + 1 - core
        return pltpu.make_async_remote_copy(
            src_ref=og.at[:, pl.ds(pl.multiple_of(tt * width, width), width)],
            dst_ref=cols.at[t],
            send_sem=up_send.at[len(near)], recv_sem=col_recv,
            device_id=device(x, y, z, 1 - core), device_id_type=MESH,
        )

    def send_up():
        for k, d, c in near:
            @pl.when(along(d) >= HALF)
            def _():
                whole(k, d, c).start()

    @pl.when(lower)
    def _():
        own_part.start()
        for d in range(1, HALF):
            for c in range(2):
                send_quarter(HALF - d, c)
        send_quarter(0, 1 - core)

    @pl.when(upper)
    def _():
        own_all.start()
        send_up()
        whole_sibling().start()

    wide[...] = jnp.zeros_like(wide)
    acc[...] = jnp.zeros_like(acc)
    pl.when(jnp.logical_not(early))(prepare)

    peers = cols.at[pl.ds(0, cols.shape[0] - 1), pl.ds(0, quarter)]
    blocks_in = cols.at[pl.ds(0, cols.shape[0] - 1)]

    def quarters(xx, lo, n):
        return cols.at[pl.ds(lo, n), pl.ds(pl.multiple_of(xx * quarter, quarter), quarter)]

    sources = cols.shape[0]
    half = sources // 2

    def pass_on(xx, lo, n, to, k):
        pltpu.make_async_remote_copy(
            src_ref=quarters(xx, lo, n), dst_ref=quarters(xx, lo, n),
            send_sem=x_send.at[k], recv_sem=x_recv.at[k],
            device_id=device(to, y, z, core), device_id_type=MESH,
        ).start()

    def passed(xx, lo, n, sem):
        pltpu.make_async_copy(quarters(xx, lo, n), quarters(xx, lo, n), sem).wait()

    opposite = (x + 2) % NX

    @pl.when(lower)
    def _():
        own_part.wait()
        pltpu.make_async_copy(peers, peers, col_recv).wait()
        pass_on(x, 0, sources, right, 0)
        pass_on(x, 0, sources, left, 1)
        pl.semaphore_wait(upper_in, 2 * jnp.where(z < 4, 4 - z, z - 3))
        send_up()
        passed(left, 0, sources, x_recv.at[0])
        pass_on(left, 0, half, right, 2)
        passed(right, 0, sources, x_recv.at[1])
        pass_on(right, half, half, left, 3)
        passed(opposite, 0, half, x_recv.at[2])
        passed(opposite, half, half, x_recv.at[3])

    @pl.when(upper)
    def _():
        own_all.wait()
        pltpu.make_async_copy(blocks_in, blocks_in, col_recv).wait()

    for copy in loads[2:]:
        copy.wait()
    grad = jnp.dot(th[...], cols[...].reshape(tokens_all, width), preferred_element_type=jnp.float32)
    grad = grad * (1.0 / math.sqrt(tokens_all))
    new_first = 0.9 * fi[...] + 0.1 * grad
    new_second = 0.95 * se[...] + 0.05 * grad * grad
    new_master = ma[...] - 0.002 * new_first / (jnp.sqrt(new_second) + 1e-08)
    wide[pl.ds(0, rows), :] = new_master

    def slot_of(ref, b, lo, n):
        return ref.at[b // NX, pl.ds(pl.multiple_of((b % NX) * SLOT + lo, 16), n)]

    w[r // NX, pl.ds(pl.multiple_of((r % NX) * SLOT, SLOT), SENT), :] = wide[pl.ds(0, SENT), :].astype(w.dtype)

    def geometry(s):
        sign = 1 - 2 * ((core + s) % 2)
        plane = (zh + s) % 2

        def block(i, j):
            xx = (x - i * sign + 2 * NX) % NX
            yy = (y - j * sign + 2 * NY) % NY
            return plane * (NX * NY) + yy * NX + xx

        def toward(axis, step):
            if axis == 0:
                return device((x + step * sign + NX) % NX, y, z, core)
            return device(x, (y + step * sign + NY) % NY, z, core)

        return block, toward

    def forward(b, part, to):
        lo, n = PARTS[part]
        pltpu.make_async_remote_copy(
            src_ref=slot_of(w, b, lo, n), dst_ref=slot_of(w, b, lo, n),
            send_sem=w_send, recv_sem=w_recv.at[b * 2 + part], device_id=to, device_id_type=MESH,
        ).start()

    def arrived(b, part):
        lo, n = PARTS[part]
        pltpu.make_async_copy(slot_of(w, b, lo, n), slot_of(w, b, lo, n), w_recv.at[b * 2 + part]).wait()

    def onward(s, i, j, part):
        block, toward = geometry(s)
        b = block(i, j)
        first_axis = 0 if part == 0 else 1
        along = (i, j)[first_axis]
        across = (i, j)[1 - first_axis]
        reach = (NX // 2, NY // 2)
        if across == 0:
            if 0 <= along < reach[first_axis]:
                forward(b, part, toward(first_axis, 1))
            if -(reach[first_axis] - 1) < along <= 0:
                forward(b, part, toward(first_axis, -1))
        if 0 <= across < reach[1 - first_axis]:
            forward(b, part, toward(1 - first_axis, 1))
        if -(reach[1 - first_axis] - 1) < across <= 0:
            forward(b, part, toward(1 - first_axis, -1))

    def wave(s, hops):
        block, _ = geometry(s)
        for i, j in offsets(hops):
            for part in ((1, 0) if i == 0 else (0, 1)):
                arrived(block(i, j), part)
                onward(s, i, j, part)

    def multiply(s, j):
        block, _ = geometry(s)
        g = block(0, j) // NX
        acc[...] += jnp.dot(apad[g], w[g], preferred_element_type=jnp.float32)

    def multiply_after(s, hops):
        j = hops - 2
        if j == 0:
            multiply(s, 0)
        elif 0 < j < NY // 2:
            def both(k, carry):
                multiply(s, j * (1 - 2 * k))
                return carry
            lax.fori_loop(0, 2, both, 0)
        elif j == NY // 2:
            multiply(s, j)

    for part in (1, 0):
        onward(0, 0, 0, part)

    zs = 4 * (1 - 2 * core)
    steps = (zs, -zs)
    for part, (lo, n) in enumerate(PARTS):
        pltpu.make_async_remote_copy(
            src_ref=slot_of(w, r, lo, n), dst_ref=relay.at[pl.ds(lo, n)],
            send_sem=z_send.at[part], recv_sem=z_recv.at[part],
            device_id=device(x, y, (z + steps[part] + NZ) % NZ, core), device_id_type=MESH,
        ).start()
    outs = [
        pltpu.make_async_copy(a, b, out_sem.at[k])
        for k, (a, b) in enumerate(((nm, nm_hbm), (nf, nf_hbm), (ns, ns_hbm)))
    ]
    nm[...] = new_master
    nf[...] = new_first
    ns[...] = new_second
    for copy in outs:
        copy.start()

    def serve_relay():
        for part, (lo, n) in enumerate(PARTS):
            origin = (z - steps[part] + NZ) % NZ
            target = (z + steps[part] + NZ) % NZ
            b = (origin // HALF) * (NX * NY) + y * NX + x
            pltpu.make_async_copy(relay.at[pl.ds(lo, n)], relay.at[pl.ds(lo, n)], z_recv.at[part]).wait()
            pltpu.make_async_remote_copy(
                src_ref=relay.at[pl.ds(lo, n)], dst_ref=slot_of(w, b, lo, n),
                send_sem=z_send.at[2 + part], recv_sem=w_recv.at[b * 2 + part],
                device_id=device(x, y, target, core), device_id_type=MESH,
            ).start()

    far = NX // 2 + NY // 2
    for hops in range(1, far + LAG):
        if hops == LAG:
            block, _ = geometry(1)
            for part in (1, 0):
                arrived(block(0, 0), part)
                onward(1, 0, 0, part)
        if hops <= far:
            wave(0, hops)
        if hops == RELAY_AFTER:
            serve_relay()
        if 1 <= hops - LAG + 1 <= far and hops >= LAG:
            wave(1, hops - LAG + 1)
        if hops <= far:
            multiply_after(0, hops)
        if 2 <= hops < 2 + NY // 2:
            relayout_plane(1 - zh, (hops - 2) * 2 * NX, 2 * NX)
        if hops >= LAG:
            multiply_after(1, hops - LAG + 1)

    dec[...] = acc[...].astype(dec.dtype)
    final = pltpu.make_async_copy(dec, dec_hbm, out_sem.at[3])
    final.start()

    @pl.when(lower)
    def _():
        pltpu.make_async_copy(peers, peers, col_send).wait()
        for k, n in enumerate((sources, sources, half, half)):
            passed(0, 0, n, x_send.at[k])

    @pl.when(upper)
    def _():
        whole_sibling().wait_send()

    for k, d, c in near:
        @pl.when(along(d) >= HALF)
        def _():
            whole(k, d, c).wait_send()

    for k in range(4):
        lo, n = PARTS[k % 2]
        pltpu.make_async_copy(relay.at[pl.ds(lo, n)], relay.at[pl.ds(lo, n)], z_send.at[k]).wait()
    window = dh.at[pl.ds(0, 2 * (NX * NY - 1) * SENT)]
    pltpu.make_async_copy(window, window, w_send).wait()
    for copy in outs:
        copy.wait()
    final.wait()


def hand_on(*refs):
    for source, target in zip(refs[:4], refs[4:]):
        target[...] = source[...]


def per_device(train_hidden, out_grad, master, first_moment, second_moment, decode_hidden):
    rows, width = master.shape
    tokens_all = train_hidden.shape[0]
    lines = decode_hidden.shape[0]
    f32, bf16 = jnp.float32, jnp.bfloat16
    any_spec = pl.BlockSpec(memory_space=pl.ANY)
    block = jax.ShapeDtypeStruct((rows, width), f32)
    groups = 2 * NY
    results = pl.pallas_call(
        kernel,
        out_shape=(block, block, block, jax.ShapeDtypeStruct((lines, width), bf16)),
        in_specs=[any_spec] * 6,
        out_specs=(any_spec,) * 4,
        scratch_shapes=[
            pltpu.VMEM((rows, tokens_all), bf16),
            pltpu.VMEM(out_grad.shape, bf16),
            pltpu.VMEM((tokens_all // out_grad.shape[0], out_grad.shape[0], width), bf16),
            pltpu.VMEM((rows, width), f32),
            pltpu.VMEM((rows, width), f32),
            pltpu.VMEM((rows, width), f32),
            pltpu.VMEM((rows, width), f32),
            pltpu.VMEM((rows, width), f32),
            pltpu.VMEM((rows, width), f32),
            pltpu.VMEM((SLOT, width), f32),
            pltpu.VMEM((decode_hidden.shape[1] + 16, lines), bf16),
            pltpu.VMEM((groups, lines, NX * SLOT), bf16),
            pltpu.VMEM((groups, NX * SLOT, width), bf16),
            pltpu.VMEM((SENT, width), bf16),
            pltpu.VMEM((lines, width), f32),
            pltpu.VMEM((lines, width), bf16),
            pltpu.SemaphoreType.DMA((6,)),
            pltpu.SemaphoreType.DMA((4,)),
            pltpu.SemaphoreType.DMA,
            pltpu.SemaphoreType.DMA,
            pltpu.SemaphoreType.DMA((4,)),
            pltpu.SemaphoreType.DMA((4,)),
            pltpu.SemaphoreType.DMA,
            pltpu.SemaphoreType.REGULAR,
            pltpu.SemaphoreType.DMA((17,)),
            pltpu.SemaphoreType.DMA,
            pltpu.SemaphoreType.DMA((2 * NX * groups,)),
            pltpu.SemaphoreType.DMA((4,)),
            pltpu.SemaphoreType.DMA((2,)),
        ],
        compiler_params=pltpu.CompilerParams(
            collective_id=0, has_side_effects=True, vmem_limit_bytes=60 * 1024 * 1024
        ),
    )(train_hidden.T, out_grad, master, first_moment, second_moment, decode_hidden.T)
    return pl.pallas_call(
        hand_on,
        out_shape=tuple(jax.ShapeDtypeStruct(a.shape, a.dtype) for a in results),
    )(*results)


def solution(mesh):
    placed = (
        P(None, "replica"),
        P("tensor", None),
        P("replica", "tensor"),
        P("replica", "tensor"),
        P("replica", "tensor"),
        P("replica", None),
    )
    return jax.shard_map(
        per_device,
        mesh=mesh,
        in_specs=placed,
        out_specs=(
            P("replica", "tensor"),
            P("replica", "tensor"),
            P("replica", "tensor"),
            P("replica", "tensor"),
        ),
        check_vma=False,
    )
```

```python
import math

import jax
import jax.numpy as jnp
from jax import lax
from jax.experimental import pallas as pl
from jax.experimental.pallas import tpu as pltpu
from jax.sharding import PartitionSpec as P

MESH = pl.DeviceIdType.MESH
NX, NY, NZ = 4, 8, 16
HALF = NZ // 2
SLOT = 256
SENT = 232
CUT = 96
PARTS = ((0, CUT), (CUT, SENT - CUT))
RELAY_AFTER = 1
LAG = 4


def offsets(hops):
    out = []
    for i in (0, 1, -1, 2):
        j = hops - abs(i)
        if j == 0:
            out.append((i, 0))
        elif j > 0:
            if j <= NY // 2:
                out.append((i, j))
            if j <= NY // 2 - 1:
                out.append((i, -j))
    return out


def kernel(
    th_hbm, og_hbm, ma_hbm, fi_hbm, se_hbm, dh_hbm,
    nm_hbm, nf_hbm, ns_hbm, dec_hbm,
    th, og, cols, ma, fi, se, nm, nf, ns, wide, dh, apad, w, relay, acc, dec,
    in_sem, out_sem, col_send, col_recv, own_sem, w_send, w_recv, z_send, z_recv,
):
    r = lax.axis_index("replica")
    t = lax.axis_index("tensor")
    x, y, zh = r % NX, (r // NX) % NY, r // (NX * NY)
    zl, core = t // 2, t % 2
    z = zh * HALF + zl
    rows, width = ma.shape
    tokens_in = og.shape[0]
    tokens_all = th.shape[1]

    def device(xx, yy, zz, cc):
        return ((zz // HALF) * (NX * NY) + yy * NX + xx, (zz % HALF) * 2 + cc)

    loads = [
        pltpu.make_async_copy(a, b, in_sem.at[k])
        for k, (a, b) in enumerate(
            ((og_hbm, og), (dh_hbm, dh.at[pl.ds(0, dh_hbm.shape[0])]), (th_hbm, th), (ma_hbm, ma), (fi_hbm, fi), (se_hbm, se))
        )
    ]
    for copy in loads:
        copy.start()

    right, left = (x + 1) % NX, (x + NX - 1) % NX
    up, down = (y + 1) % NY, (y + NY - 1) % NY
    barrier = pltpu.get_barrier_semaphore()
    greeted = [device(right, y, z, core), device(left, y, z, core),
               device(x, up, z, core), device(x, down, z, core), device(x, y, z, 1 - core)]
    for d in (4, -4, 3, -3, 2, -2, 1, -1):
        for c in range(2):
            greeted.append(device(x, y, (z + d + NZ) % NZ, c))
    for d in reversed(greeted):
        pl.semaphore_signal(barrier, inc=1, device_id=d, device_id_type=MESH)
    pl.semaphore_wait(barrier, len(greeted))

    loads[0].wait()
    first = pl.multiple_of(zl * 2 * tokens_in + core * tokens_in, tokens_in)
    own = pltpu.make_async_copy(
        og.at[:, pl.ds(pl.multiple_of(t * width, width), width)],
        cols.at[pl.ds(first, tokens_in)], own_sem)
    own.start()

    def send_columns(d, c, lo, n):
        zz = (z + d + NZ) % NZ
        tt = (zz % HALF) * 2 + c
        pltpu.make_async_remote_copy(
            src_ref=og.at[pl.ds(lo, n), pl.ds(pl.multiple_of(tt * width, width), width)],
            dst_ref=cols.at[pl.ds(pl.multiple_of(first + lo, n), n)],
            send_sem=col_send, recv_sem=col_recv,
            device_id=device(x, y, zz, c), device_id_type=MESH,
        ).start()

    half = tokens_in // 2
    for c in range(2):
        send_columns(4, c, 0, half)
        send_columns(-4, c, half, half)
    for d in (3, -3, 2, -2, 1, -1):
        for c in range(2):
            send_columns(d, c, 0, tokens_in)
    send_columns(0, 1 - core, 0, tokens_in)

    wide[...] = jnp.zeros_like(wide)
    acc[...] = jnp.zeros_like(acc)

    def clear(g, carry):
        for k in range(NX):
            w[g, pl.ds(k * SLOT + SENT, SLOT - SENT), :] = jnp.zeros((SLOT - SENT, width), w.dtype)
        return carry

    lax.fori_loop(0, w.shape[0], clear, 0)
    loads[1].wait()
    lane = lax.broadcasted_iota(jnp.int32, (128, 128), 1)

    def relayout(b, carry):
        base = pl.multiple_of((b * rows) // 16 * 16, 16)
        shift = b * rows - base
        at = pl.multiple_of((b % NX) * SLOT, SLOT)
        for s in range(0, dh.shape[1], 128):
            tile = dh[pl.ds(base, SLOT), pl.ds(s, 128)].T.astype(jnp.float32)
            turned = [pltpu.roll(tile[:, k * 128 : k * 128 + 128], (128 - shift) % 128, 1) for k in range(2)]
            low = jnp.where(lane < 128 - shift, turned[0], turned[1])
            high = jnp.where(lane < rows - 128, turned[1], 0.0)
            apad[b // NX, pl.ds(s, 128), pl.ds(at, 128)] = low.astype(apad.dtype)
            apad[b // NX, pl.ds(s, 128), pl.ds(pl.multiple_of(at + 128, 128), 128)] = high.astype(apad.dtype)
        return carry

    lax.fori_loop(0, NX * w.shape[0], relayout, 0)

    for copy in loads[2:]:
        copy.wait()
    own.wait()
    others = tokens_all - tokens_in
    pltpu.make_async_copy(cols.at[pl.ds(0, others)], cols.at[pl.ds(0, others)], col_recv).wait()
    grad = jnp.dot(th[...], cols[...], preferred_element_type=jnp.float32)
    grad = grad * (1.0 / math.sqrt(tokens_all))
    new_first = 0.9 * fi[...] + 0.1 * grad
    new_second = 0.95 * se[...] + 0.05 * grad * grad
    new_master = ma[...] - 0.002 * new_first / (jnp.sqrt(new_second) + 1e-08)
    wide[pl.ds(0, rows), :] = new_master

    def slot_of(ref, b, lo, n):
        return ref.at[b // NX, pl.ds(pl.multiple_of((b % NX) * SLOT + lo, 16), n)]

    w[r // NX, pl.ds(pl.multiple_of((r % NX) * SLOT, SLOT), SENT), :] = wide[pl.ds(0, SENT), :].astype(w.dtype)

    def geometry(s):
        sign = 1 - 2 * ((core + s) % 2)
        plane = (zh + s) % 2

        def block(i, j):
            xx = (x - i * sign + 2 * NX) % NX
            yy = (y - j * sign + 2 * NY) % NY
            return plane * (NX * NY) + yy * NX + xx

        def toward(axis, step):
            if axis == 0:
                return device((x + step * sign + NX) % NX, y, z, core)
            return device(x, (y + step * sign + NY) % NY, z, core)

        return block, toward

    def forward(b, part, to):
        lo, n = PARTS[part]
        pltpu.make_async_remote_copy(
            src_ref=slot_of(w, b, lo, n), dst_ref=slot_of(w, b, lo, n),
            send_sem=w_send, recv_sem=w_recv.at[b * 2 + part], device_id=to, device_id_type=MESH,
        ).start()

    def arrived(b, part):
        lo, n = PARTS[part]
        pltpu.make_async_copy(slot_of(w, b, lo, n), slot_of(w, b, lo, n), w_recv.at[b * 2 + part]).wait()

    def onward(s, i, j, part):
        block, toward = geometry(s)
        b = block(i, j)
        first_axis = 0 if part == 0 else 1
        along = (i, j)[first_axis]
        across = (i, j)[1 - first_axis]
        reach = (NX // 2, NY // 2)
        if across == 0:
            if 0 <= along < reach[first_axis]:
                forward(b, part, toward(first_axis, 1))
            if -(reach[first_axis] - 1) < along <= 0:
                forward(b, part, toward(first_axis, -1))
        if 0 <= across < reach[1 - first_axis]:
            forward(b, part, toward(1 - first_axis, 1))
        if -(reach[1 - first_axis] - 1) < across <= 0:
            forward(b, part, toward(1 - first_axis, -1))

    def wave(s, hops):
        block, _ = geometry(s)
        for i, j in offsets(hops):
            for part in ((1, 0) if i == 0 else (0, 1)):
                arrived(block(i, j), part)
                onward(s, i, j, part)

    def multiply(s, j):
        block, _ = geometry(s)
        g = block(0, j) // NX
        acc[...] += jnp.dot(apad[g], w[g], preferred_element_type=jnp.float32)

    def multiply_after(s, hops):
        j = hops - 2
        if j == 0:
            multiply(s, 0)
        elif 0 < j < NY // 2:
            def both(k, carry):
                multiply(s, j * (1 - 2 * k))
                return carry
            lax.fori_loop(0, 2, both, 0)
        elif j == NY // 2:
            multiply(s, j)

    zs = 4 * (1 - 2 * core)
    steps = (zs, -zs)
    for part, (lo, n) in enumerate(PARTS):
        pltpu.make_async_remote_copy(
            src_ref=slot_of(w, r, lo, n), dst_ref=relay.at[pl.ds(lo, n)],
            send_sem=z_send.at[part], recv_sem=z_recv.at[part],
            device_id=device(x, y, (z + steps[part] + NZ) % NZ, core), device_id_type=MESH,
        ).start()
    for part in (1, 0):
        onward(0, 0, 0, part)
    outs = [
        pltpu.make_async_copy(a, b, out_sem.at[k])
        for k, (a, b) in enumerate(((nm, nm_hbm), (nf, nf_hbm), (ns, ns_hbm)))
    ]
    nm[...] = new_master
    nf[...] = new_first
    ns[...] = new_second
    for copy in outs:
        copy.start()

    def serve_relay():
        for part, (lo, n) in enumerate(PARTS):
            origin = (z - steps[part] + NZ) % NZ
            target = (z + steps[part] + NZ) % NZ
            b = (origin // HALF) * (NX * NY) + y * NX + x
            pltpu.make_async_copy(relay.at[pl.ds(lo, n)], relay.at[pl.ds(lo, n)], z_recv.at[part]).wait()
            pltpu.make_async_remote_copy(
                src_ref=relay.at[pl.ds(lo, n)], dst_ref=slot_of(w, b, lo, n),
                send_sem=z_send.at[2 + part], recv_sem=w_recv.at[b * 2 + part],
                device_id=device(x, y, target, core), device_id_type=MESH,
            ).start()

    far = NX // 2 + NY // 2
    for hops in range(1, far + LAG):
        if hops == LAG:
            block, _ = geometry(1)
            for part in (1, 0):
                arrived(block(0, 0), part)
                onward(1, 0, 0, part)
        if hops <= far:
            wave(0, hops)
        if hops == RELAY_AFTER:
            serve_relay()
        if 1 <= hops - LAG + 1 <= far and hops >= LAG:
            wave(1, hops - LAG + 1)
        if hops <= far:
            multiply_after(0, hops)
        if hops >= LAG:
            multiply_after(1, hops - LAG + 1)

    dec[...] = acc[...].astype(dec.dtype)
    final = pltpu.make_async_copy(dec, dec_hbm, out_sem.at[3])
    final.start()

    pltpu.make_async_copy(cols.at[pl.ds(0, others)], cols.at[pl.ds(0, others)], col_send).wait()
    for k in range(4):
        lo, n = PARTS[k % 2]
        pltpu.make_async_copy(relay.at[pl.ds(lo, n)], relay.at[pl.ds(lo, n)], z_send.at[k]).wait()
    window = dh.at[pl.ds(0, 2 * (NX * NY - 1) * SENT)]
    pltpu.make_async_copy(window, window, w_send).wait()
    for copy in outs:
        copy.wait()
    final.wait()


def hand_on(*refs):
    for source, target in zip(refs[:4], refs[4:]):
        target[...] = source[...]


def per_device(train_hidden, out_grad, master, first_moment, second_moment, decode_hidden):
    rows, width = master.shape
    tokens_all = train_hidden.shape[0]
    lines = decode_hidden.shape[0]
    f32, bf16 = jnp.float32, jnp.bfloat16
    any_spec = pl.BlockSpec(memory_space=pl.ANY)
    block = jax.ShapeDtypeStruct((rows, width), f32)
    groups = 2 * NY
    results = pl.pallas_call(
        kernel,
        out_shape=(block, block, block, jax.ShapeDtypeStruct((lines, width), bf16)),
        in_specs=[any_spec] * 6,
        out_specs=(any_spec,) * 4,
        scratch_shapes=[
            pltpu.VMEM((rows, tokens_all), bf16),
            pltpu.VMEM(out_grad.shape, bf16),
            pltpu.VMEM((tokens_all, width), bf16),
            pltpu.VMEM((rows, width), f32),
            pltpu.VMEM((rows, width), f32),
            pltpu.VMEM((rows, width), f32),
            pltpu.VMEM((rows, width), f32),
            pltpu.VMEM((rows, width), f32),
            pltpu.VMEM((rows, width), f32),
            pltpu.VMEM((SLOT, width), f32),
            pltpu.VMEM((decode_hidden.shape[1] + 16, lines), bf16),
            pltpu.VMEM((groups, lines, NX * SLOT), bf16),
            pltpu.VMEM((groups, NX * SLOT, width), bf16),
            pltpu.VMEM((SENT, width), bf16),
            pltpu.VMEM((lines, width), f32),
            pltpu.VMEM((lines, width), bf16),
            pltpu.SemaphoreType.DMA((6,)),
            pltpu.SemaphoreType.DMA((4,)),
            pltpu.SemaphoreType.DMA,
            pltpu.SemaphoreType.DMA,
            pltpu.SemaphoreType.DMA,
            pltpu.SemaphoreType.DMA,
            pltpu.SemaphoreType.DMA((2 * NX * groups,)),
            pltpu.SemaphoreType.DMA((4,)),
            pltpu.SemaphoreType.DMA((2,)),
        ],
        compiler_params=pltpu.CompilerParams(
            collective_id=0, has_side_effects=True, vmem_limit_bytes=60 * 1024 * 1024
        ),
    )(train_hidden.T, out_grad, master, first_moment, second_moment, decode_hidden.T)
    return pl.pallas_call(
        hand_on,
        out_shape=tuple(jax.ShapeDtypeStruct(a.shape, a.dtype) for a in results),
    )(*results)


def solution(mesh):
    placed = (
        P(None, "replica"),
        P("tensor", None),
        P("replica", "tensor"),
        P("replica", "tensor"),
        P("replica", "tensor"),
        P("replica", None),
    )
    return jax.shard_map(
        per_device,
        mesh=mesh,
        in_specs=placed,
        out_specs=(
            P("replica", "tensor"),
            P("replica", "tensor"),
            P("replica", "tensor"),
            P("replica", "tensor"),
        ),
        check_vma=False,
    )
```
